512 devices in a mesh: dp: 32 (over x, y_lo, core), mp: 16 (over z, y_hi).
Axes of the slice: x: 4, y: 8 (y_hi: 2, y_lo: 4; y = y_hi * 4 + y_lo), z: 8, core: 2. Of those that a mesh axis runs over, the one named last changes fastest.
Arguments:
- features: bfloat16 [57344, 1024], P(('dp', 'mp')), may hold values from -6 to 6
- row_position: int32 [57344], P(('dp', 'mp')), may hold values from 0 to 2047, as said below
- proj_weight: bfloat16 [1024, 8192], P(None, 'mp'), may hold values from -0.1875 to 0.1875
- proj_bias: float32 [8192], P('mp'), may hold values from -3 to 3
- norm_gain: float32 [8192], replicated, may hold values from 0.5 to 1.5
- cotangent: bfloat16 [65536, 8192], P(('dp', 'mp')), may hold values from -0.03125 to 0.03125
Outputs:
- grad_weight: bfloat16 [1024, 8192], P(None, 'mp')
- grad_bias: float32 [8192], P('mp')
The draws below stay inside these ranges and needn't reach their ends.
Inputs may be any that keep to these rules, and one draw needn't show every extreme that they name: `row_position`: within each sequence's block of 1792 entries the positions are distinct; every such block holds position 0 and position 2047.
All inputs are finite; a program needn't handle non-finite values.
Results may differ from the reference program's by a relative error of at most 0.0059.
Values may be sent and summed in bfloat16 or wider, within the bound.
No kernel may reach another device: no remote copies, remote signals or barrier semaphores. Data moves between devices by JAX's collectives and lax.ppermute only.
A program may use at most 64 MiB of HBM per device.

```python
import jax
import jax.numpy as jnp
from jax import lax

VIS = 1024
D = 8192
SEQ = 2048
IMG_ROWS = 1792
N_DP = 32


def draw_row_position(key, part):

    def one_group(group_key):
        first_key, second_key = jax.random.split(group_key)
        middle = 1 + jax.random.permutation(first_key, SEQ - 2)[:IMG_ROWS - 2]
        chosen = jnp.concatenate([jnp.array([0, SEQ - 1], jnp.int32), middle.astype(jnp.int32)])
        return chosen[jax.random.permutation(second_key, IMG_ROWS)]
    group_keys = jax.random.split(jax.random.fold_in(key, 7), N_DP)
    return jax.vmap(one_group)(group_keys).reshape(-1).astype(jnp.int32)


def shard_levels(own_key, extent, shards, low, largest):
    level = 1.0
    for position, blocks in shards:
        steps = jax.random.uniform(jax.random.fold_in(jax.random.fold_in(own_key, 6), position), (blocks,), jnp.float32, low / len(shards), largest / len(shards))
        level = level * jnp.repeat(jnp.exp(steps), extent[position] // blocks).reshape((-1,) + (1,) * (len(extent) - 1 - position))
    return level


def noise(stream_key, shape, deviation, bound, cuts=(), dtype=jnp.bfloat16):
    result = jax.random.normal(stream_key, shape, jnp.float32) * deviation
    if len(cuts) > 0:
        result = shard_levels(stream_key, shape, cuts, -0.22, 0.18) * result
    return jnp.clip(result, min=-bound, max=bound).astype(dtype)


def setup_inputs(seed: int = 0) -> dict:
    arg_keys = jax.random.split(jax.random.key(seed), 7)
    features = noise(arg_keys[0], (N_DP * IMG_ROWS, VIS), 1.0, 6.0, ((0, 512),))
    row_position = draw_row_position(jax.random.fold_in(arg_keys[6], 71), 0)
    proj_weight = noise(arg_keys[2], (VIS, D), VIS ** -0.5, 0.1875, ((1, 16),))
    proj_bias = noise(arg_keys[3], (D,), 0.5, 3.0, ((0, 16),), jnp.float32)
    norm_gain = jnp.clip(1.0 + 0.1 * jax.random.normal(arg_keys[4], (D,), jnp.float32), 0.5, 1.5)
    cotangent = noise(arg_keys[5], (N_DP * SEQ, D), (1.25 * (N_DP * IMG_ROWS) ** -0.5), 0.03125, ((0, 512),))
    return {"features": features, "row_position": row_position, "proj_weight": proj_weight, "proj_bias": proj_bias, "norm_gain": norm_gain, "cotangent": cotangent}


EPSILON = 1e-05

def gelu_pair(pre_act):
    normal_cdf = 0.5 * (1.0 + lax.erf(pre_act * 0.7071067811865476))
    normal_pdf = jnp.exp(-0.5 * pre_act * pre_act) * 0.3989422804014327
    return (pre_act * normal_cdf, normal_cdf + pre_act * normal_pdf)

def reference(features, row_position, proj_weight, proj_bias, norm_gain, cotangent):
    group_feats = features.reshape(N_DP, IMG_ROWS, VIS)
    group_pos = row_position.reshape(N_DP, IMG_ROWS)
    group_cot = cotangent.reshape(N_DP, SEQ, D)

    def one_group(carry, inputs):
        feats, places, cot_rows = inputs
        places = places.astype(jnp.int32)
        pre_act = jnp.dot(feats, proj_weight, preferred_element_type=jnp.float32) + proj_bias
        activated, slope = gelu_pair(pre_act)
        projected = activated.astype(jnp.bfloat16)
        embed = jnp.zeros((SEQ, D), jnp.bfloat16).at[places].set(projected)
        embed_wide = lax.optimization_barrier(embed).astype(jnp.float32)
        inv_rms = lax.rsqrt(lax.optimization_barrier(jnp.mean(embed_wide * embed_wide, axis=1, keepdims=True)) + EPSILON)
        scaled_cot = cot_rows.astype(jnp.float32) * norm_gain
        gdot = lax.optimization_barrier(jnp.mean(scaled_cot * embed_wide, axis=1, keepdims=True))
        grad_embed = (inv_rms * scaled_cot - embed_wide * inv_rms * inv_rms * inv_rms * gdot).astype(jnp.bfloat16)
        grad_proj = lax.optimization_barrier(grad_embed[places]).astype(jnp.float32)
        grad_pre = (grad_proj * slope).astype(jnp.bfloat16)
        weight_grad = lax.dot_general(feats, grad_pre, (((0,), (0,)), ((), ())), preferred_element_type=jnp.float32)
        bias_grad = lax.optimization_barrier(jnp.sum(grad_pre.astype(jnp.float32), axis=0))
        return ((carry[0] + weight_grad, carry[1] + bias_grad), None)
    start = (jnp.zeros((VIS, D), jnp.float32), jnp.zeros((D,), jnp.float32))
    (weight_grad, bias_grad), _ = lax.scan(one_group, start, (group_feats, group_pos, group_cot))
    return (weight_grad.astype(jnp.bfloat16), bias_grad)
```

```python
import jax
import jax.numpy as jnp
from jax import lax
from jax.sharding import Mesh, PartitionSpec as P

EPSILON = 1e-05
DP = ("x", "yl", "c")
MP = ("z", "yh")
XY = ("x", "yl")
f32 = jnp.float32
bf16 = jnp.bfloat16


def gelu_pair(pre_act):
    normal_cdf = 0.5 * (1.0 + lax.erf(pre_act * 0.7071067811865476))
    normal_pdf = jnp.exp(-0.5 * pre_act * pre_act) * 0.3989422804014327
    return (pre_act * normal_cdf, normal_cdf + pre_act * normal_pdf)


def swap(value, axis):
    return lax.ppermute(value, axis, [(0, 1), (1, 0)])


def exchange(blocks, axes):
    return lax.all_to_all(blocks, axes, split_axis=0, concat_axis=0)


def spread(block, axes, count):
    return exchange(jnp.broadcast_to(block[None], (count,) + block.shape), axes)


def per_device(features, row_position, proj_weight, proj_bias, norm_gain, cotangent):
    rows = features.shape[0]
    vis, width = proj_weight.shape
    nz, nx, ny = lax.axis_size("z"), lax.axis_size("x"), lax.axis_size("yl")
    nm = 2 * nz
    chips = nx * ny
    seq_rows, features_out = cotangent.shape
    total = rows * nm
    z, yh, c = lax.axis_index("z"), lax.axis_index("yh"), lax.axis_index("c")
    me = z * 2 + yh

    blocks = cotangent.reshape(seq_rows, nm, width).transpose(1, 0, 2)
    cot = exchange(blocks, MP).reshape(nm * seq_rows, width)

    own = lax.all_gather(features, "z", axis=0, tiled=True)
    other = lax.all_gather(swap(features, "yh"), "z", axis=0, tiled=True)

    padded = jnp.pad(row_position, (0, 1024 - rows)).reshape(8, 128)
    places = spread(padded, MP, nm).reshape(nz, 2, 1024)[:, :, :rows]
    places = jnp.where(yh == 0, places, places[:, ::-1])
    places = places.transpose(1, 0, 2).reshape(2, nz * rows)

    gain = lax.dynamic_slice(norm_gain, (me * width,), (width,))
    halves = []
    for feats, where in ((own, places[0]), (other, places[1])):
        pre_act = jnp.dot(feats, proj_weight, preferred_element_type=f32) + proj_bias
        activated, slope = gelu_pair(pre_act)
        projected = activated.astype(bf16)
        hot = (where[:, None] == jnp.arange(nm * seq_rows)[None, :]).astype(bf16)
        picked = jnp.dot(hot, cot, preferred_element_type=f32)
        scaled = picked * gain
        wide = projected.astype(f32)
        squares = jnp.sum(wide * wide, axis=1)
        dots = jnp.sum(scaled * wide, axis=1)
        halves.append((feats, slope, wide, scaled, squares, dots))

    per_half = nz * rows
    stats = jnp.stack(
        [jnp.where(yh == 0, jnp.stack([halves[0][k], halves[1][k]]), jnp.stack([halves[1][k], halves[0][k]])) for k in (4, 5)]
    )
    stats = jnp.pad(stats.reshape(-1), (0, 4096 - 4 * per_half)).reshape(32, 128)
    stats = jnp.sum(spread(stats, MP, nm), axis=0).reshape(-1)[: 4 * per_half]
    stats = stats.reshape(2, 2, per_half) / features_out
    stats = jnp.where(yh == 0, stats, stats[:, ::-1])

    weight_grad = jnp.zeros((vis, width), f32)
    bias_grad = jnp.zeros((width,), f32)
    for k, (feats, slope, wide, scaled, _, _) in enumerate(halves):
        inv_rms = lax.rsqrt(stats[0, k] + EPSILON)[:, None]
        gdot = stats[1, k][:, None]
        grad_embed = (inv_rms * scaled - wide * (inv_rms * inv_rms * inv_rms * gdot)).astype(bf16)
        grad_pre = (grad_embed.astype(f32) * slope).astype(bf16)
        bias_grad = bias_grad + jnp.sum(grad_pre.astype(f32), axis=0)
        weight_grad = weight_grad + lax.dot_general(
            feats, grad_pre, (((0,), (0,)), ((), ())), preferred_element_type=f32
        )

    half = vis // 2
    kept = lax.dynamic_slice(weight_grad, (c * half, 0), (half, width))
    sent = lax.dynamic_slice(weight_grad, ((1 - c) * half, 0), (half, width)).astype(bf16)
    chip = (kept + swap(sent, "c").astype(f32)).astype(bf16)
    piece = exchange(chip.reshape(chips, half // chips, width), XY)
    piece = jnp.sum(piece.astype(f32), axis=0).astype(bf16)
    high = bias_grad.astype(bf16)
    low = (bias_grad - high.astype(f32)).astype(bf16)
    row = lax.broadcasted_iota(jnp.int32, (8, width), 0)
    tail = jnp.where(row == 0, high[None], jnp.where(row == 1, low[None], jnp.zeros((), bf16)))
    full = spread(jnp.concatenate([piece, tail], axis=0), XY, chips)
    mine = full[:, : half // chips].reshape(half, width)
    bias = jnp.sum(full[:, half // chips : half // chips + 2].astype(f32), axis=(0, 1))
    high = bias.astype(bf16)
    low = (bias - high.astype(f32)).astype(bf16)
    tail = jnp.where(row == 0, high[None], jnp.where(row == 1, low[None], jnp.zeros((), bf16)))
    theirs = swap(jnp.concatenate([mine, tail], axis=0), "c")
    bias = bias + jnp.sum(theirs[half : half + 2].astype(f32), axis=0)
    theirs = theirs[:half]
    first = jnp.where(c == 0, mine, theirs)
    second = jnp.where(c == 0, theirs, mine)
    return (jnp.concatenate([first, second], axis=0), bias)


def solution(mesh):
    parts = Mesh(mesh.devices.reshape(4, 4, 2, 8, 2), DP + MP)
    return jax.shard_map(
        per_device,
        mesh=parts,
        in_specs=(
            P(DP + MP, None),
            P(DP + MP),
            P(None, MP),
            P(MP),
            P(),
            P(DP + MP, None),
        ),
        out_specs=(P(None, MP), P(MP)),
        check_vma=False,
    )
```

```python
import functools

import jax
import jax.numpy as jnp
from jax import lax
from jax.experimental import pallas as pl
from jax.experimental.pallas import tpu as pltpu
from jax.sharding import Mesh, PartitionSpec as P


EPSILON = 1e-05
DP = ("x", "yl", "c")
MP = ("z", "yh")
XY = ("x", "yl")
f32 = jnp.float32
bf16 = jnp.bfloat16
TILE = 256
LANES = 128
EARLY = 32
HEAD = 8
MIB = 1024 * 1024


def swap(value, axis):
    return lax.ppermute(value, axis, [(0, 1), (1, 0)])


def exchange(blocks, axes):
    return lax.all_to_all(blocks, axes, split_axis=0, concat_axis=0)


def spread(block, axes, count):
    return exchange(jnp.broadcast_to(block[None], (count,) + block.shape), axes)


def params(mib):
    return pltpu.CompilerParams(vmem_limit_bytes=mib * MIB)


def pick_kernel(index_ref, early_ref, late_ref, picked_ref):
    index = index_ref[...]
    total = jnp.zeros(picked_ref.shape, f32)
    start = 0
    for source in (early_ref, late_ref):
        depth = source.shape[0]
        columns = lax.broadcasted_iota(jnp.int32, (index.shape[0], depth), 1) + start
        hot = jnp.where(columns == index, 1.0, 0.0).astype(bf16)
        total = total + jnp.dot(hot, source[...], preferred_element_type=f32)
        start += depth
    picked_ref[...] = total.astype(bf16)


def pick(index, early, late):
    total, width = index.shape[0], early.shape[1]
    return pl.pallas_call(
        pick_kernel,
        grid=(total // TILE,),
        in_specs=[
            pl.BlockSpec((TILE, 1), lambda i: (i, 0)),
            pl.BlockSpec(early.shape, lambda i: (0, 0)),
            pl.BlockSpec(late.shape, lambda i: (0, 0)),
        ],
        out_specs=pl.BlockSpec((TILE, width), lambda i: (i, 0)),
        out_shape=jax.ShapeDtypeStruct((total, width), bf16),
        compiler_params=params(16),
        cost_estimate=pl.CostEstimate(
            flops=2 * total * (early.shape[0] + late.shape[0]) * width, bytes_accessed=6 << 20, transcendentals=0
        ),
        name="pick",
    )(index, early, late)


def project_kernel(feats_ref, weight_ref, bias_ref, gain_ref, picked_ref, proj_ref, slope_ref, stats_ref):
    step = pl.program_id(0)
    value = jnp.dot(feats_ref[...], weight_ref[...], preferred_element_type=f32) + bias_ref[...]
    cdf = 0.5 * (1.0 + lax.erf(value * 0.7071067811865476))
    pdf = jnp.exp(-0.5 * value * value) * 0.3989422804014327
    slope_ref[...] = cdf + value * pdf
    projected = (value * cdf).astype(bf16)
    proj_ref[...] = projected
    wide = projected.astype(f32)
    squares = jnp.sum(wide * wide, axis=1, keepdims=True)
    dots = jnp.sum(picked_ref[...].astype(f32) * gain_ref[...] * wide, axis=1, keepdims=True)

    @pl.when(step == 0)
    def _():
        stats_ref[...] = jnp.zeros_like(stats_ref)

    lane = lax.broadcasted_iota(jnp.int32, (LANES, LANES), 1)
    parts = TILE // LANES
    for part in range(parts):
        rows = slice(part * LANES, (part + 1) * LANES)
        both = jnp.where(lane == 0, squares[rows], dots[rows]).T
        row = step * parts + part
        stats_ref[pl.ds(row, 1), :] = both[0:1]
        stats_ref[pl.ds(stats_ref.shape[0] // 2 + row, 1), :] = both[1:2]


def project(feats, weight, bias, gain, picked):
    total, vis = feats.shape
    width = weight.shape[1]
    stat_rows = 2 * (-(-total // LANES // 8) * 8)
    return pl.pallas_call(
        project_kernel,
        grid=(total // TILE,),
        in_specs=[
            pl.BlockSpec((TILE, vis), lambda i: (i, 0)),
            pl.BlockSpec((vis, width), lambda i: (0, 0)),
            pl.BlockSpec((1, width), lambda i: (0, 0)),
            pl.BlockSpec((1, width), lambda i: (0, 0)),
            pl.BlockSpec((TILE, width), lambda i: (i, 0)),
        ],
        out_specs=[
            pl.BlockSpec((TILE, width), lambda i: (i, 0)),
            pl.BlockSpec((TILE, width), lambda i: (i, 0)),
            pl.BlockSpec((stat_rows, LANES), lambda i: (0, 0)),
        ],
        out_shape=[
            jax.ShapeDtypeStruct((total, width), bf16),
            jax.ShapeDtypeStruct((total, width), f32),
            jax.ShapeDtypeStruct((stat_rows, LANES), f32),
        ],
        compiler_params=params(61),
        cost_estimate=pl.CostEstimate(flops=2 * total * vis * width, bytes_accessed=10 << 20, transcendentals=total * width),
        name="project",
    )(feats, weight, bias, gain, picked)


def backward_kernel(
    core_ref, feats_ref, gain_ref, picked_ref, proj_ref, slope_ref, stats_ref, sent_ref, kept_ref, bias_ref, acc, bias_acc, sums,
    *, features_out, pieces
):
    step = pl.program_id(0)

    @pl.when(step == 0)
    def _():
        acc[...] = jnp.zeros_like(acc)
        bias_acc[...] = jnp.zeros_like(bias_acc)
        means = jnp.sum(stats_ref[...], axis=0) / features_out
        half = means.shape[0] // 2
        inv_rms = lax.rsqrt(means[:half] + EPSILON)
        sums[:half] = inv_rms
        sums[half:] = inv_rms * inv_rms * inv_rms * means[half:]

    parts = TILE // LANES
    half = sums.shape[0] // 2
    width = proj_ref.shape[1]
    grads = []
    for part in range(parts):
        rows = slice(part * LANES, (part + 1) * LANES)
        row = step * parts + part
        inv_rms = jnp.broadcast_to(sums[pl.ds(row, 1), :], (LANES, LANES)).T
        factor = jnp.broadcast_to(sums[pl.ds(half + row, 1), :], (LANES, LANES)).T
        columns = []
        for j in range(width // LANES):
            cols = slice(j * LANES, (j + 1) * LANES)
            scaled = picked_ref[rows, cols].astype(f32) * gain_ref[:, cols]
            grad = (inv_rms * scaled - proj_ref[rows, cols].astype(f32) * factor).astype(bf16)
            columns.append((grad.astype(f32) * slope_ref[rows, cols]).astype(bf16))
        grads.append(jnp.concatenate(columns, axis=1))
    grad_pre = jnp.concatenate(grads, axis=0)
    bias_acc[...] += jnp.sum(grad_pre.astype(f32).reshape(TILE // 8, 8, width), axis=0)
    acc[...] += lax.dot_general(feats_ref[...], grad_pre, (((0,), (0,)), ((), ())), preferred_element_type=f32)

    @pl.when(step == pl.num_programs(0) - 1)
    def _():
        vis = acc.shape[0]
        rows = vis // 2 // pieces
        core = core_ref[0]
        for piece in range(pieces):
            for j in range(width // LANES):
                cols = slice(j * LANES, (j + 1) * LANES)
                at = (piece * (width // LANES) + j) * rows
                mine = pl.multiple_of(core * (vis // 2) + piece * rows, 8)
                other = pl.multiple_of((1 - core) * (vis // 2) + piece * rows, 8)
                kept_ref[at : at + rows, :] = acc[pl.ds(mine, rows), cols]
                sent_ref[at : at + rows, :] = acc[pl.ds(other, rows), cols].astype(bf16)
        bias = jnp.sum(bias_acc[...], axis=0, keepdims=True)
        lines = jnp.concatenate([bias[:, j * LANES : (j + 1) * LANES] for j in range(width // LANES)], axis=0)
        bias_ref[...] = lines
        high = lines.astype(bf16).astype(f32)
        both = jnp.concatenate([high, lines - high], axis=0).astype(bf16)
        sent_ref[sent_ref.shape[0] - 2 * lines.shape[0] :, :] = both


def backward(core, feats, gain, picked, proj, slope, stats, features_out, pieces):
    total, vis = feats.shape
    width = proj.shape[1]
    lines = width // LANES
    out_rows = vis // 2 * lines
    return pl.pallas_call(
        functools.partial(backward_kernel, features_out=features_out, pieces=pieces),
        grid_spec=pltpu.PrefetchScalarGridSpec(
            num_scalar_prefetch=1,
            grid=(total // TILE,),
            in_specs=[
                pl.BlockSpec((TILE, vis), lambda i, c: (i, 0)),
                pl.BlockSpec((1, width), lambda i, c: (0, 0)),
                pl.BlockSpec((TILE, width), lambda i, c: (i, 0)),
                pl.BlockSpec((TILE, width), lambda i, c: (i, 0)),
                pl.BlockSpec((TILE, width), lambda i, c: (i, 0)),
                pl.BlockSpec(stats.shape, lambda i, c: (0, 0, 0)),
            ],
            out_specs=[
                pl.BlockSpec((out_rows + 2 * lines, LANES), lambda i, c: (0, 0)),
                pl.BlockSpec((out_rows, LANES), lambda i, c: (0, 0)),
                pl.BlockSpec((lines, LANES), lambda i, c: (0, 0)),
            ],
            scratch_shapes=[
                pltpu.VMEM((vis, width), f32),
                pltpu.VMEM((8, width), f32),
                pltpu.VMEM(stats.shape[1:], f32),
            ],
        ),
        out_shape=[
            jax.ShapeDtypeStruct((out_rows + 2 * lines, LANES), bf16),
            jax.ShapeDtypeStruct((out_rows, LANES), f32),
            jax.ShapeDtypeStruct((lines, LANES), f32),
        ],
        compiler_params=params(61),
        cost_estimate=pl.CostEstimate(flops=2 * total * vis * width, bytes_accessed=10 << 20, transcendentals=0),
        name="backward",
    )(core, feats, gain, picked, proj, slope, stats)


def assemble_kernel(core_ref, mine_ref, theirs_ref, grad_ref, bias_ref, *, size):
    core = core_ref[0]
    pieces = mine_ref.shape[0]
    vis, width = grad_ref.shape
    lines = width // LANES
    rows = size // lines
    for piece in range(pieces):
        for j in range(lines):
            cols = slice(j * LANES, (j + 1) * LANES)
            part = slice(j * rows, (j + 1) * rows)
            for half, ref in ((core, mine_ref), (1 - core, theirs_ref)):
                at = pl.multiple_of(half * (vis // 2) + piece * rows, rows)
                grad_ref[pl.ds(at, rows), cols] = ref[piece, part, :]
    both = jnp.sum(mine_ref[:, size:, :].astype(f32), axis=0)
    bias_ref[...] = both[:lines] + both[lines:]


def assemble(core, mine, theirs, vis, width, size):
    return pl.pallas_call(
        functools.partial(assemble_kernel, size=size),
        in_specs=[
            pl.BlockSpec(memory_space=pltpu.SMEM),
            pl.BlockSpec(memory_space=pltpu.VMEM),
            pl.BlockSpec(memory_space=pltpu.VMEM),
        ],
        out_specs=[pl.BlockSpec(memory_space=pltpu.VMEM), pl.BlockSpec(memory_space=pltpu.VMEM)],
        out_shape=[jax.ShapeDtypeStruct((vis, width), bf16), jax.ShapeDtypeStruct((width // LANES, LANES), f32)],
        compiler_params=params(8),
        cost_estimate=pl.CostEstimate(flops=0, bytes_accessed=2 << 20, transcendentals=0),
        name="assemble",
    )(core, mine, theirs)


def per_device(features, row_position, proj_weight, proj_bias, norm_gain, cotangent):
    rows = features.shape[0]
    vis, width = proj_weight.shape
    nz, nx, ny = lax.axis_size("z"), lax.axis_size("x"), lax.axis_size("yl")
    nm = 2 * nz
    chips = nx * ny
    seq_rows, features_out = cotangent.shape
    total = rows * nm
    z, yh, c = lax.axis_index("z"), lax.axis_index("yh"), lax.axis_index("c")
    me = z * 2 + yh
    partner = swap(features, "yh")
    digits = jnp.stack([row_position // LANES, row_position % LANES]).astype(bf16)
    digits = jnp.pad(digits, ((0, HEAD - 2), (0, width - rows)))
    blocks = cotangent.reshape(seq_rows, nm, width)
    early = jnp.concatenate([jnp.broadcast_to(digits[:, None], (HEAD, nm, width)), blocks[:EARLY]], axis=0)
    early = exchange(early.transpose(1, 0, 2), MP)
    pair = jnp.concatenate([features, partner], axis=0)
    pair = jnp.where(yh == 0, pair, jnp.concatenate([partner, features], axis=0))
    pair, late = lax.optimization_barrier((pair, blocks[EARLY:].transpose(1, 0, 2)))
    feats = lax.all_gather(pair, "z", axis=0, tiled=True)
    late = exchange(late, MP)

    digits = early[:, :2, :rows].astype(jnp.int32)
    places = (digits[:, 0] * LANES + digits[:, 1]).reshape(total, 1)
    owner, offset = places // seq_rows, places % seq_rows
    index = jnp.where(
        offset < EARLY,
        owner * (HEAD + EARLY) + HEAD + offset,
        nm * (HEAD + EARLY) + owner * (seq_rows - EARLY) + offset - EARLY,
    )
    picked = pick(index, early.reshape(-1, width), late.reshape(-1, width))

    gain = lax.dynamic_slice(norm_gain, (me * width,), (width,))[None]
    proj, slope, stats = project(feats, proj_weight, proj_bias[None], gain, picked)
    stats = spread(stats, MP, nm)
    core = c.astype(jnp.int32)[None]
    sent, kept, bias = backward(core, feats, gain, picked, proj, slope, stats, features_out, chips)

    lines = width // LANES
    got = swap(sent, "c")
    size = kept.shape[0]
    chip = (kept + got[:size].astype(f32)).astype(bf16)
    bias = bias + got[size : size + lines].astype(f32) + got[size + lines :].astype(f32)
    piece = exchange(chip.reshape(chips, size // chips, LANES), XY)
    piece = jnp.sum(piece.astype(f32), axis=0).astype(bf16)
    high = bias.astype(bf16)
    low = (bias - high.astype(f32)).astype(bf16)
    full = spread(jnp.concatenate([piece, high, low], axis=0), XY, chips)
    theirs = swap(full, "c")
    grad, bias = assemble(core, full, theirs, vis, width, size // chips)
    return (grad, bias.reshape(width))


def solution(mesh):
    parts = Mesh(mesh.devices.reshape(4, 4, 2, 8, 2), DP + MP)
    return jax.shard_map(
        per_device,
        mesh=parts,
        in_specs=(P(DP + MP, None), P(DP + MP), P(None, MP), P(MP), P(), P(DP + MP, None)),
        out_specs=(P(None, MP), P(MP)),
        check_vma=False,
    )
```

```python
import functools

import jax
import jax.numpy as jnp
from jax import lax
from jax.experimental import pallas as pl
from jax.experimental.pallas import tpu as pltpu
from jax.sharding import Mesh, PartitionSpec as P


EPSILON = 1e-05
DP = ("x", "yl", "c")
MP = ("z", "yh")
XY = ("x", "yl")
f32 = jnp.float32
bf16 = jnp.bfloat16
TILE = 256
DEEP = 896
LANES = 128
EARLY = 32
HEAD = 8
MIB = 1024 * 1024


def swap(value, axis):
    return lax.ppermute(value, axis, [(0, 1), (1, 0)])


def exchange(blocks, axes):
    return lax.all_to_all(blocks, axes, split_axis=0, concat_axis=0)


def spread(block, axes, count):
    return exchange(jnp.broadcast_to(block[None], (count,) + block.shape), axes)


def params(mib):
    return pltpu.CompilerParams(vmem_limit_bytes=mib * MIB)


def pick_kernel(index_ref, early_ref, late_ref, picked_ref):
    index = index_ref[...]
    total = jnp.zeros(picked_ref.shape, f32)
    start = 0
    for source in (early_ref, late_ref):
        depth = source.shape[0]
        columns = lax.broadcasted_iota(jnp.int32, (index.shape[0], depth), 1) + start
        hot = jnp.where(columns == index, 1.0, 0.0).astype(bf16)
        total = total + jnp.dot(hot, source[...], preferred_element_type=f32)
        start += depth
    picked_ref[...] = total.astype(bf16)


def pick(index, early, late):
    total, width = index.shape[0], early.shape[1]
    return pl.pallas_call(
        pick_kernel,
        grid=(total // TILE,),
        in_specs=[
            pl.BlockSpec((TILE, 1), lambda i: (i, 0)),
            pl.BlockSpec(early.shape, lambda i: (0, 0)),
            pl.BlockSpec(late.shape, lambda i: (0, 0)),
        ],
        out_specs=pl.BlockSpec((TILE, width), lambda i: (i, 0)),
        out_shape=jax.ShapeDtypeStruct((total, width), bf16),
        compiler_params=params(16),
        cost_estimate=pl.CostEstimate(
            flops=2 * total * (early.shape[0] + late.shape[0]) * width, bytes_accessed=6 << 20, transcendentals=0
        ),
        name="pick",
    )(index, early, late)


def project_kernel(feats_ref, weight_ref, bias_ref, gain_ref, picked_ref, proj_ref, slope_ref, stats_ref, sums):
    step = pl.program_id(0)
    value = jnp.dot(feats_ref[...], weight_ref[...], preferred_element_type=f32) + bias_ref[...]
    cdf = 0.5 * (1.0 + lax.erf(value * 0.7071067811865476))
    pdf = jnp.exp(-0.5 * value * value) * 0.3989422804014327
    slope_ref[...] = cdf + value * pdf
    projected = (value * cdf).astype(bf16)
    proj_ref[...] = projected
    wide = projected.astype(f32)
    squares = jnp.sum(wide * wide, axis=1, keepdims=True)
    dots = jnp.sum(picked_ref[...].astype(f32) * gain_ref[...] * wide, axis=1, keepdims=True)

    @pl.when(step == 0)
    def _():
        sums[...] = jnp.zeros_like(sums)

    lane = lax.broadcasted_iota(jnp.int32, (LANES, LANES), 1)
    parts = TILE // LANES
    for part in range(parts):
        rows = slice(part * LANES, (part + 1) * LANES)
        both = jnp.where(lane == 0, squares[rows], dots[rows]).T
        row = step * parts + part
        sums[pl.ds(row, 1), :] = both[0:1]
        sums[pl.ds(sums.shape[0] // 2 + row, 1), :] = both[1:2]

    @pl.when(step == pl.num_programs(0) - 1)
    def _():
        stats_ref[...] = jnp.broadcast_to(sums[...][None], stats_ref.shape)


def project(feats, weight, bias, gain, picked, copies):
    total, vis = feats.shape
    width = weight.shape[1]
    stat_rows = 2 * (-(-total // LANES // 8) * 8)
    return pl.pallas_call(
        project_kernel,
        grid=(total // TILE,),
        in_specs=[
            pl.BlockSpec((TILE, vis), lambda i: (i, 0)),
            pl.BlockSpec((vis, width), lambda i: (0, 0)),
            pl.BlockSpec((1, width), lambda i: (0, 0)),
            pl.BlockSpec((1, width), lambda i: (0, 0)),
            pl.BlockSpec((TILE, width), lambda i: (i, 0)),
        ],
        out_specs=[
            pl.BlockSpec((TILE, width), lambda i: (i, 0)),
            pl.BlockSpec((TILE, width), lambda i: (i, 0)),
            pl.BlockSpec((copies, stat_rows, LANES), lambda i: (0, 0, 0)),
        ],
        out_shape=[
            pltpu.HBM((total, width), bf16),
            pltpu.HBM((total, width), f32),
            jax.ShapeDtypeStruct((copies, stat_rows, LANES), f32),
        ],
        scratch_shapes=[pltpu.VMEM((stat_rows, LANES), f32)],
        compiler_params=params(24),
        cost_estimate=pl.CostEstimate(flops=2 * total * vis * width, bytes_accessed=10 << 20, transcendentals=total * width),
        name="project",
    )(feats, weight, bias, gain, picked)


def backward_kernel(
    core_ref, feats_ref, gain_ref, picked_ref, proj_ref, slope_ref, stats_ref, sent_ref, kept_ref, bias_ref, acc, bias_acc, sums,
    *, features_out, pieces
):
    step = pl.program_id(0)

    @pl.when(step == 0)
    def _():
        acc[...] = jnp.zeros_like(acc)
        bias_acc[...] = jnp.zeros_like(bias_acc)
        means = jnp.sum(stats_ref[...], axis=0) / features_out
        half = means.shape[0] // 2
        inv_rms = lax.rsqrt(means[:half] + EPSILON)
        sums[:half] = inv_rms
        sums[half:] = inv_rms * inv_rms * inv_rms * means[half:]

    parts = DEEP // LANES
    half = sums.shape[0] // 2
    width = proj_ref.shape[1]
    grads = []
    for part in range(parts):
        rows = slice(part * LANES, (part + 1) * LANES)
        row = step * parts + part
        inv_rms = jnp.broadcast_to(sums[pl.ds(row, 1), :], (LANES, LANES)).T
        factor = jnp.broadcast_to(sums[pl.ds(half + row, 1), :], (LANES, LANES)).T
        columns = []
        for j in range(width // LANES):
            cols = slice(j * LANES, (j + 1) * LANES)
            scaled = picked_ref[rows, cols].astype(f32) * gain_ref[:, cols]
            grad = (inv_rms * scaled - proj_ref[rows, cols].astype(f32) * factor).astype(bf16)
            columns.append((grad.astype(f32) * slope_ref[rows, cols]).astype(bf16))
        grads.append(jnp.concatenate(columns, axis=1))
    grad_pre = jnp.concatenate(grads, axis=0)
    bias_acc[...] += jnp.sum(grad_pre.astype(f32).reshape(DEEP // 8, 8, width), axis=0)
    acc[...] += lax.dot_general(feats_ref[...], grad_pre, (((0,), (0,)), ((), ())), preferred_element_type=f32)

    @pl.when(step == pl.num_programs(0) - 1)
    def _():
        vis = acc.shape[0]
        rows = vis // 2 // pieces
        core = core_ref[0]
        for piece in range(pieces):
            for j in range(width // LANES):
                cols = slice(j * LANES, (j + 1) * LANES)
                at = (piece * (width // LANES) + j) * rows
                mine = pl.multiple_of(core * (vis // 2) + piece * rows, 8)
                other = pl.multiple_of((1 - core) * (vis // 2) + piece * rows, 8)
                kept_ref[at : at + rows, :] = acc[pl.ds(mine, rows), cols]
                sent_ref[at : at + rows, :] = acc[pl.ds(other, rows), cols].astype(bf16)
        bias = jnp.sum(bias_acc[...], axis=0, keepdims=True)
        lines = jnp.concatenate([bias[:, j * LANES : (j + 1) * LANES] for j in range(width // LANES)], axis=0)
        bias_ref[...] = lines
        high = lines.astype(bf16).astype(f32)
        both = jnp.concatenate([high, lines - high], axis=0).astype(bf16)
        sent_ref[sent_ref.shape[0] - 2 * lines.shape[0] :, :] = both


def backward(core, feats, gain, picked, proj, slope, stats, features_out, pieces):
    total, vis = feats.shape
    width = proj.shape[1]
    lines = width // LANES
    out_rows = vis // 2 * lines
    return pl.pallas_call(
        functools.partial(backward_kernel, features_out=features_out, pieces=pieces),
        grid_spec=pltpu.PrefetchScalarGridSpec(
            num_scalar_prefetch=1,
            grid=(total // DEEP,),
            in_specs=[
                pl.BlockSpec((DEEP, vis), lambda i, c: (i, 0)),
                pl.BlockSpec((1, width), lambda i, c: (0, 0)),
                pl.BlockSpec((DEEP, width), lambda i, c: (i, 0)),
                pl.BlockSpec((DEEP, width), lambda i, c: (i, 0)),
                pl.BlockSpec((DEEP, width), lambda i, c: (i, 0)),
                pl.BlockSpec(stats.shape, lambda i, c: (0, 0, 0)),
            ],
            out_specs=[
                pl.BlockSpec((out_rows + 2 * lines, LANES), lambda i, c: (0, 0)),
                pl.BlockSpec((out_rows, LANES), lambda i, c: (0, 0)),
                pl.BlockSpec((lines, LANES), lambda i, c: (0, 0)),
            ],
            scratch_shapes=[
                pltpu.VMEM((vis, width), f32),
                pltpu.VMEM((8, width), f32),
                pltpu.VMEM(stats.shape[1:], f32),
            ],
        ),
        out_shape=[
            jax.ShapeDtypeStruct((out_rows + 2 * lines, LANES), bf16),
            jax.ShapeDtypeStruct((out_rows, LANES), f32),
            jax.ShapeDtypeStruct((lines, LANES), f32),
        ],
        compiler_params=params(24),
        cost_estimate=pl.CostEstimate(flops=2 * total * vis * width, bytes_accessed=10 << 20, transcendentals=0),
        name="backward",
    )(core, feats, gain, picked, proj, slope, stats)


def assemble_kernel(core_ref, mine_ref, theirs_ref, grad_ref, bias_ref, *, size):
    core = core_ref[0]
    pieces = mine_ref.shape[0]
    vis, width = grad_ref.shape
    lines = width // LANES
    rows = size // lines
    for piece in range(pieces):
        for j in range(lines):
            cols = slice(j * LANES, (j + 1) * LANES)
            part = slice(j * rows, (j + 1) * rows)
            for half, ref in ((core, mine_ref), (1 - core, theirs_ref)):
                at = pl.multiple_of(half * (vis // 2) + piece * rows, rows)
                grad_ref[pl.ds(at, rows), cols] = ref[piece, part, :]
    both = jnp.sum(mine_ref[:, size:, :].astype(f32), axis=0)
    bias_ref[...] = both[:lines] + both[lines:]


def assemble(core, mine, theirs, vis, width, size):
    return pl.pallas_call(
        functools.partial(assemble_kernel, size=size),
        in_specs=[
            pl.BlockSpec(memory_space=pltpu.SMEM),
            pl.BlockSpec(memory_space=pltpu.VMEM),
            pl.BlockSpec(memory_space=pltpu.VMEM),
        ],
        out_specs=[pl.BlockSpec(memory_space=pltpu.VMEM), pl.BlockSpec(memory_space=pltpu.VMEM)],
        out_shape=[jax.ShapeDtypeStruct((vis, width), bf16), jax.ShapeDtypeStruct((width // LANES, LANES), f32)],
        compiler_params=params(8),
        cost_estimate=pl.CostEstimate(flops=0, bytes_accessed=2 << 20, transcendentals=0),
        name="assemble",
    )(core, mine, theirs)


def per_device(features, row_position, proj_weight, proj_bias, norm_gain, cotangent):
    rows = features.shape[0]
    vis, width = proj_weight.shape
    nz, nx, ny = lax.axis_size("z"), lax.axis_size("x"), lax.axis_size("yl")
    nm = 2 * nz
    chips = nx * ny
    seq_rows, features_out = cotangent.shape
    total = rows * nm
    z, yh, c = lax.axis_index("z"), lax.axis_index("yh"), lax.axis_index("c")
    me = z * 2 + yh
    partner = swap(features, "yh")
    digits = jnp.stack([row_position // LANES, row_position % LANES]).astype(bf16)
    digits = jnp.pad(digits, ((0, HEAD - 2), (0, width - rows)))
    blocks = cotangent.reshape(seq_rows, nm, width)
    early = jnp.concatenate([jnp.broadcast_to(digits[:, None], (HEAD, nm, width)), blocks[:EARLY]], axis=0)
    early = exchange(early.transpose(1, 0, 2), MP)
    pair = jnp.concatenate([features, partner], axis=0)
    pair = jnp.where(yh == 0, pair, jnp.concatenate([partner, features], axis=0))
    pair, blocks = lax.optimization_barrier((pair, blocks))
    late = blocks[EARLY:].transpose(1, 0, 2)
    feats = pltpu.with_memory_space_constraint(lax.all_gather(pair, "z", axis=0, tiled=True), pltpu.HBM)
    late = exchange(late, MP)

    digits = early[:, :2, :rows].astype(jnp.int32)
    places = (digits[:, 0] * LANES + digits[:, 1]).reshape(total, 1)
    owner, offset = places // seq_rows, places % seq_rows
    index = jnp.where(
        offset < EARLY,
        owner * (HEAD + EARLY) + HEAD + offset,
        nm * (HEAD + EARLY) + owner * (seq_rows - EARLY) + offset - EARLY,
    )
    picked = pick(index, early.reshape(-1, width), late.reshape(-1, width))

    gain = lax.dynamic_slice(norm_gain, (me * width,), (width,))[None]
    proj, slope, stats = project(feats, proj_weight, proj_bias[None], gain, picked, nm)
    stats = exchange(stats, MP)
    proj, slope = (pltpu.with_memory_space_constraint(value, pltpu.HBM) for value in (proj, slope))
    core = c.astype(jnp.int32)[None]
    sent, kept, bias = backward(core, feats, gain, picked, proj, slope, stats, features_out, chips)

    lines = width // LANES
    got = swap(sent, "c")
    size = kept.shape[0]
    chip = (kept + got[:size].astype(f32)).astype(bf16)
    bias = bias + got[size : size + lines].astype(f32) + got[size + lines :].astype(f32)
    piece = exchange(chip.reshape(chips, size // chips, LANES), XY)
    piece = jnp.sum(piece.astype(f32), axis=0).astype(bf16)
    high = bias.astype(bf16)
    low = (bias - high.astype(f32)).astype(bf16)
    full = spread(jnp.concatenate([piece, high, low], axis=0), XY, chips)
    theirs = swap(full, "c")
    grad, bias = assemble(core, full, theirs, vis, width, size // chips)
    return (grad, bias.reshape(width))


def solution(mesh):
    parts = Mesh(mesh.devices.reshape(4, 4, 2, 8, 2), DP + MP)
    return jax.shard_map(
        per_device,
        mesh=parts,
        in_specs=(P(DP + MP, None), P(DP + MP), P(None, MP), P(MP), P(), P(DP + MP, None)),
        out_specs=(P(None, MP), P(MP)),
        check_vma=False,
    )
```

```python
import functools

import jax
import jax.numpy as jnp
from jax import lax
from jax.experimental import pallas as pl
from jax.experimental.pallas import tpu as pltpu
from jax.sharding import Mesh, PartitionSpec as P


EPSILON = 1e-05
DP = ("x", "yl", "c")
MP = ("z", "yh")
XY = ("x", "yl")
f32 = jnp.float32
bf16 = jnp.bfloat16
TILE = 256
DEEP = 896
LANES = 128
EARLY = 32
HEAD = 8
MIB = 1024 * 1024


def swap(value, axis):
    return lax.ppermute(value, axis, [(0, 1), (1, 0)])


def exchange(blocks, axes):
    return lax.all_to_all(blocks, axes, split_axis=0, concat_axis=0)


def spread(block, axes, count):
    return exchange(jnp.broadcast_to(block[None], (count,) + block.shape), axes)


def stay(value):
    return pltpu.with_memory_space_constraint(value, pltpu.HBM)


def params(mib):
    return pltpu.CompilerParams(vmem_limit_bytes=mib * MIB)


def pick_kernel(index_ref, early_ref, late_ref, picked_ref):
    index = index_ref[...]
    total = jnp.zeros(picked_ref.shape, f32)
    start = 0
    for source in (early_ref, late_ref):
        depth = source.shape[0]
        columns = lax.broadcasted_iota(jnp.int32, (index.shape[0], depth), 1) + start
        hot = jnp.where(columns == index, 1.0, 0.0).astype(bf16)
        total = total + jnp.dot(hot, source[...], preferred_element_type=f32)
        start += depth
    picked_ref[...] = total.astype(bf16)


def pick(index, early, late):
    total, width = index.shape[0], early.shape[1]
    return pl.pallas_call(
        pick_kernel,
        grid=(total // TILE,),
        in_specs=[
            pl.BlockSpec((TILE, 1), lambda i: (i, 0)),
            pl.BlockSpec(early.shape, lambda i: (0, 0)),
            pl.BlockSpec(late.shape, lambda i: (0, 0)),
        ],
        out_specs=pl.BlockSpec((TILE, width), lambda i: (i, 0)),
        out_shape=jax.ShapeDtypeStruct((total, width), bf16),
        compiler_params=params(16),
        cost_estimate=pl.CostEstimate(
            flops=2 * total * (early.shape[0] + late.shape[0]) * width, bytes_accessed=6 << 20, transcendentals=0
        ),
        name="pick",
    )(index, early, late)


def project_kernel(feats_ref, weight_ref, bias_ref, gain_ref, picked_ref, proj_ref, slope_ref, stats_ref, sums):
    step = pl.program_id(0)
    value = jnp.dot(feats_ref[...], weight_ref[...], preferred_element_type=f32) + bias_ref[...]
    cdf = 0.5 * (1.0 + lax.erf(value * 0.7071067811865476))
    pdf = jnp.exp(-0.5 * value * value) * 0.3989422804014327
    slope_ref[...] = cdf + value * pdf
    projected = (value * cdf).astype(bf16)
    proj_ref[...] = projected
    wide = projected.astype(f32)
    squares = jnp.sum(wide * wide, axis=1, keepdims=True)
    dots = jnp.sum(picked_ref[...].astype(f32) * gain_ref[...] * wide, axis=1, keepdims=True)

    @pl.when(step == 0)
    def _():
        sums[...] = jnp.zeros_like(sums)

    lane = lax.broadcasted_iota(jnp.int32, (LANES, LANES), 1)
    parts = TILE // LANES
    for part in range(parts):
        rows = slice(part * LANES, (part + 1) * LANES)
        both = jnp.where(lane == 0, squares[rows], dots[rows]).T
        row = step * parts + part
        sums[pl.ds(row, 1), :] = both[0:1]
        sums[pl.ds(sums.shape[0] // 2 + row, 1), :] = both[1:2]

    @pl.when(step == pl.num_programs(0) - 1)
    def _():
        stats_ref[...] = jnp.broadcast_to(sums[...][None], stats_ref.shape)


def project(feats, weight, bias, gain, picked, copies):
    total, vis = feats.shape
    width = weight.shape[1]
    stat_rows = 2 * (-(-total // LANES // 8) * 8)
    return pl.pallas_call(
        project_kernel,
        grid=(total // TILE,),
        in_specs=[
            pl.BlockSpec((TILE, vis), lambda i: (i, 0)),
            pl.BlockSpec((vis, width), lambda i: (0, 0)),
            pl.BlockSpec((1, width), lambda i: (0, 0)),
            pl.BlockSpec((1, width), lambda i: (0, 0)),
            pl.BlockSpec((TILE, width), lambda i: (i, 0)),
        ],
        out_specs=[
            pl.BlockSpec((TILE, width), lambda i: (i, 0)),
            pl.BlockSpec((TILE, width), lambda i: (i, 0)),
            pl.BlockSpec((copies, stat_rows, LANES), lambda i: (0, 0, 0)),
        ],
        out_shape=[
            jax.ShapeDtypeStruct((total, width), bf16),
            jax.ShapeDtypeStruct((total, width), f32),
            jax.ShapeDtypeStruct((copies, stat_rows, LANES), f32),
        ],
        scratch_shapes=[pltpu.VMEM((stat_rows, LANES), f32)],
        compiler_params=params(24),
        cost_estimate=pl.CostEstimate(flops=2 * total * vis * width, bytes_accessed=10 << 20, transcendentals=total * width),
        name="project",
    )(feats, weight, bias, gain, picked)


def backward_kernel(
    core_ref, feats_ref, gain_ref, picked_ref, proj_ref, slope_ref, stats_ref, sent_ref, kept_ref, bias_ref, acc, sums,
    *, features_out, pieces
):
    means = jnp.sum(stats_ref[...], axis=0) / features_out
    half = means.shape[0] // 2
    inv_rms = lax.rsqrt(means[:half] + EPSILON)
    sums[:half] = inv_rms
    sums[half:] = inv_rms * inv_rms * inv_rms * means[half:]
    vis, width = acc.shape
    bias = jnp.zeros((8, width), f32)
    for step in range(feats_ref.shape[0] // DEEP):
        grads = []
        for part in range(DEEP // LANES):
            row = step * (DEEP // LANES) + part
            rows = slice(row * LANES, (row + 1) * LANES)
            inv_rms = jnp.broadcast_to(sums[row : row + 1, :], (LANES, LANES)).T
            factor = jnp.broadcast_to(sums[half + row : half + row + 1, :], (LANES, LANES)).T
            columns = []
            for j in range(width // LANES):
                cols = slice(j * LANES, (j + 1) * LANES)
                scaled = picked_ref[rows, cols].astype(f32) * gain_ref[:, cols]
                grad = (inv_rms * scaled - proj_ref[rows, cols].astype(f32) * factor).astype(bf16)
                columns.append((grad.astype(f32) * slope_ref[rows, cols]).astype(bf16))
            grads.append(jnp.concatenate(columns, axis=1))
        grad_pre = jnp.concatenate(grads, axis=0)
        bias = bias + jnp.sum(grad_pre.astype(f32).reshape(DEEP // 8, 8, width), axis=0)
        feats = feats_ref[step * DEEP : (step + 1) * DEEP, :]
        part = lax.dot_general(feats, grad_pre, (((0,), (0,)), ((), ())), preferred_element_type=f32)
        acc[...] = part if step == 0 else acc[...] + part

    rows = vis // 2 // pieces
    core = core_ref[0]
    for piece in range(pieces):
        for j in range(width // LANES):
            cols = slice(j * LANES, (j + 1) * LANES)
            at = (piece * (width // LANES) + j) * rows
            mine = pl.multiple_of(core * (vis // 2) + piece * rows, 8)
            other = pl.multiple_of((1 - core) * (vis // 2) + piece * rows, 8)
            kept_ref[at : at + rows, :] = acc[pl.ds(mine, rows), cols]
            sent_ref[at : at + rows, :] = acc[pl.ds(other, rows), cols].astype(bf16)
    bias = jnp.sum(bias, axis=0, keepdims=True)
    lines = jnp.concatenate([bias[:, j * LANES : (j + 1) * LANES] for j in range(width // LANES)], axis=0)
    bias_ref[...] = lines
    high = lines.astype(bf16).astype(f32)
    sent_ref[sent_ref.shape[0] - 2 * lines.shape[0] :, :] = jnp.concatenate([high, lines - high], axis=0).astype(bf16)


def backward(core, feats, gain, picked, proj, slope, stats, features_out, pieces):
    total, vis = feats.shape
    width = proj.shape[1]
    lines = width // LANES
    out_rows = vis // 2 * lines
    vmem = pl.BlockSpec(memory_space=pltpu.VMEM)
    return pl.pallas_call(
        functools.partial(backward_kernel, features_out=features_out, pieces=pieces),
        in_specs=[pl.BlockSpec(memory_space=pltpu.SMEM)] + [vmem] * 6,
        out_specs=[vmem] * 3,
        out_shape=[
            jax.ShapeDtypeStruct((out_rows + 2 * lines, LANES), bf16),
            jax.ShapeDtypeStruct((out_rows, LANES), f32),
            jax.ShapeDtypeStruct((lines, LANES), f32),
        ],
        scratch_shapes=[pltpu.VMEM((vis, width), f32), pltpu.VMEM(stats.shape[1:], f32)],
        compiler_params=params(24),
        cost_estimate=pl.CostEstimate(flops=2 * total * vis * width, bytes_accessed=10 << 20, transcendentals=0),
        name="backward",
    )(core, feats, gain, picked, proj, slope, stats)


def assemble_kernel(core_ref, mine_ref, theirs_ref, grad_ref, bias_ref, *, size):
    core = core_ref[0]
    pieces = mine_ref.shape[0]
    vis, width = grad_ref.shape
    lines = width // LANES
    rows = size // lines
    for piece in range(pieces):
        for j in range(lines):
            cols = slice(j * LANES, (j + 1) * LANES)
            part = slice(j * rows, (j + 1) * rows)
            for half, ref in ((core, mine_ref), (1 - core, theirs_ref)):
                at = pl.multiple_of(half * (vis // 2) + piece * rows, rows)
                grad_ref[pl.ds(at, rows), cols] = ref[piece, part, :]
    both = jnp.sum(mine_ref[:, size:, :].astype(f32), axis=0)
    bias_ref[...] = both[:lines] + both[lines:]


def assemble(core, mine, theirs, vis, width, size):
    return pl.pallas_call(
        functools.partial(assemble_kernel, size=size),
        in_specs=[
            pl.BlockSpec(memory_space=pltpu.SMEM),
            pl.BlockSpec(memory_space=pltpu.VMEM),
            pl.BlockSpec(memory_space=pltpu.VMEM),
        ],
        out_specs=[pl.BlockSpec(memory_space=pltpu.VMEM), pl.BlockSpec(memory_space=pltpu.VMEM)],
        out_shape=[jax.ShapeDtypeStruct((vis, width), bf16), jax.ShapeDtypeStruct((width // LANES, LANES), f32)],
        compiler_params=params(8),
        cost_estimate=pl.CostEstimate(flops=0, bytes_accessed=2 << 20, transcendentals=0),
        name="assemble",
    )(core, mine, theirs)


def per_device(features, row_position, proj_weight, proj_bias, norm_gain, cotangent):
    rows = features.shape[0]
    vis, width = proj_weight.shape
    nz, nx, ny = lax.axis_size("z"), lax.axis_size("x"), lax.axis_size("yl")
    nm = 2 * nz
    chips = nx * ny
    seq_rows, features_out = cotangent.shape
    total = rows * nm
    z, yh, c = lax.axis_index("z"), lax.axis_index("yh"), lax.axis_index("c")
    me = (z * 2 + yh) * width
    low_half = yh == 0
    core = c.astype(jnp.int32)[None]
    partner = swap(features, "yh")
    row_position, me, low_half, core = lax.optimization_barrier((row_position, me, low_half, core))
    digits = jnp.stack([row_position // LANES, row_position % LANES]).astype(bf16)
    digits = jnp.pad(digits, ((0, HEAD - 2), (0, width - rows)))
    blocks = cotangent.reshape(seq_rows, nm, width)
    early = jnp.concatenate([jnp.broadcast_to(digits[:, None], (HEAD, nm, width)), blocks[:EARLY]], axis=0)
    early = exchange(early.transpose(1, 0, 2), MP)
    pair = jnp.concatenate([features, partner], axis=0)
    pair = jnp.where(low_half, pair, jnp.concatenate([partner, features], axis=0))
    pair, blocks = lax.optimization_barrier((pair, blocks))
    late = blocks[EARLY:].transpose(1, 0, 2)
    feats = lax.all_gather(pair, "z", axis=0, tiled=True)
    late = exchange(late, MP)

    digits = early[:, :2, :rows].astype(jnp.int32)
    places = (digits[:, 0] * LANES + digits[:, 1]).reshape(total, 1)
    owner, offset = places // seq_rows, places % seq_rows
    index = jnp.where(
        offset < EARLY,
        owner * (HEAD + EARLY) + HEAD + offset,
        nm * (HEAD + EARLY) + owner * (seq_rows - EARLY) + offset - EARLY,
    )
    picked = pick(index, early.reshape(-1, width), late.reshape(-1, width))

    gain = lax.dynamic_slice(norm_gain, (me,), (width,))[None]
    proj, slope, stats = project(stay(feats), stay(proj_weight), proj_bias[None], gain, picked, nm)
    stats = exchange(stats, MP)
    sent, kept, bias = backward(core, feats, gain, picked, proj, slope, stats, features_out, chips)

    lines = width // LANES
    got = swap(sent, "c")
    size = kept.shape[0]
    chip = (kept + got[:size].astype(f32)).astype(bf16)
    bias = bias + got[size : size + lines].astype(f32) + got[size + lines :].astype(f32)
    piece = exchange(chip.reshape(chips, size // chips, LANES), XY)
    piece = jnp.sum(piece.astype(f32), axis=0).astype(bf16)
    high = bias.astype(bf16)
    low = (bias - high.astype(f32)).astype(bf16)
    full = spread(jnp.concatenate([piece, high, low], axis=0), XY, chips)
    theirs = swap(full, "c")
    grad, bias = assemble(core, full, theirs, vis, width, size // chips)
    return (grad, bias.reshape(width))


def solution(mesh):
    parts = Mesh(mesh.devices.reshape(4, 4, 2, 8, 2), DP + MP)
    return jax.shard_map(
        per_device,
        mesh=parts,
        in_specs=(P(DP + MP, None), P(DP + MP), P(None, MP), P(MP), P(), P(DP + MP, None)),
        out_specs=(P(None, MP), P(MP)),
        check_vma=False,
    )
```
